32 devices in a mesh: scen: 8 (over z, x), row: 2 (over y), col: 2 (over core).
Axes of the slice: x: 2, y: 2, z: 4, core: 2. Of those that a mesh axis runs over, the one named last changes fastest.
Arguments:
- coupling: bfloat16 [24, 512, 3072], P('scen', None, ('row', 'col')), may hold values from -0.078125 to 0.078125
- factor_inv: bfloat16 [24, 512, 512], P('scen'), as said below
- block_mask: int32 [24, 4, 24], P('scen', None, ('row', 'col')), may hold values 0 or 1
Outputs:
- schur: float32 [2, 1536, 2, 2, 768], P('row', 'scen', None, 'col')
The draws below stay inside these ranges and needn't reach their ends.
Inputs may be any that keep to these rules, and one draw needn't show every extreme that they name: factor_inv is lower triangular with a positive diagonal.
All inputs are finite; a program needn't handle non-finite values. No bound on the sum of `block_mask` on one device may be relied on, other than what follows from the above.
Results may differ from the reference program's by a relative error of at most 0.00064.
Values may be sent and summed in bfloat16 or wider, within the bound.
A program may use at most 64 MiB of HBM per device.

```python
import jax
import jax.numpy as jnp
from jax import lax

NB = 512
NS = 3072
BLK = 128
SCENS = 24
N_ROW = 2
N_COL = 2


def draw_factor_inv(key, part):
    first, second = jax.random.split(key)
    rows = jnp.arange(NB)[:, None]
    cols = jnp.arange(NB)[None, :]
    lower = (cols < rows).astype(jnp.float32)
    eye = (cols == rows).astype(jnp.float32)
    off = jax.random.normal(first, (SCENS, NB, NB), jnp.float32)
    diag = jax.random.uniform(second, (SCENS, NB, 1), jnp.float32, 0.5, 1.5)
    value = off * lower * NB ** (-0.5) + eye * diag
    return value.astype(jnp.bfloat16)


def touch_ends(entries, key, least, largest):
    spot = [jax.random.randint(jax.random.fold_in(key, axis), (), 0, length) for axis, length in enumerate(entries.shape)]
    longest = entries.shape.index(max(entries.shape))
    beside = spot[:longest] + [(spot[longest] + 1) % entries.shape[longest]] + spot[longest + 1:]
    return entries.at[tuple(spot)].set(least).at[tuple(beside)].set(largest)


def with_spikes(result, own_key, source, target, blocks, factor):
    owner, partner = [(jnp.arange(result.shape[position]) // (result.shape[position] // blocks)).reshape([-1 if axis == position else 1 for axis in range(result.ndim)]) for position in (source, target)]
    chosen = jax.random.permutation(own_key, blocks)[partner]
    strong = (owner == chosen) | (owner == (partner + blocks // 2) % blocks)
    return jnp.where(strong, factor * result, result)


def block_levels(rng, shape, shards, smallest, top_value):
    def one(position, parts):
        draws = jax.random.uniform(jax.random.fold_in(jax.random.fold_in(rng, 6), position), (parts,), jnp.float32, smallest / len(shards), top_value / len(shards))
        return jnp.repeat(jnp.exp(draws), shape[position] // parts).reshape((-1,) + (1,) * (len(shape) - position - 1))

    factor_of = one(*shards[0])
    for cut in shards[1:]:
        factor_of = factor_of * one(*cut)
    return factor_of


def heavy_noise(stream_key, dims, deviation, limit, cuts, heavy, held_as=jnp.bfloat16):
    entries = deviation * jax.random.normal(stream_key, dims, jnp.float32)
    if cuts:
        entries = entries * block_levels(stream_key, dims, cuts, -0.22, 0.18)
    return jnp.clip(with_spikes(entries, jax.random.fold_in(stream_key, 3), *heavy), -limit, limit).astype(held_as)


def setup_inputs(seed: int = 0) -> dict:
    splits = jax.random.split(jax.random.key(seed), 4)
    return {
        "coupling": heavy_noise(splits[0], (SCENS, NB, NS), (NB * SCENS) ** -0.5, 0.078125, ((0, 8), (2, 4)), (0, 2, 8, 2.0)),
        "factor_inv": draw_factor_inv(jax.random.fold_in(splits[3], 71), 0),
        "block_mask": touch_ends((jax.random.randint(splits[2], (SCENS, NB // BLK, NS // BLK), 0, 2) < 1).astype(jnp.int32), jax.random.fold_in(splits[2], 1), 0, 1),
    }


def reference(coupling, factor_inv, block_mask):
    def step(total, items):
        block, factor, pattern = items
        spread = jnp.broadcast_to(pattern[:, None, :, None], (NB // BLK, BLK, NS // BLK, BLK)).reshape(NB, NS)
        masked = block * spread.astype(jnp.bfloat16)
        solved = jnp.dot(factor, masked, preferred_element_type=jnp.float32).astype(jnp.bfloat16)
        product = lax.dot_general(solved, solved, (((0,), (0,)), ((), ())), preferred_element_type=jnp.float32)
        return total + product, None

    start = jnp.zeros((NS, NS), jnp.float32)
    total, unused = lax.scan(step, start, (coupling, factor_inv, block_mask))
    return total.reshape(N_ROW, NS // N_ROW, N_ROW, N_COL, NS // (N_ROW * N_COL))
```

```python
import functools

import jax
import jax.numpy as jnp
from jax import lax
from jax.experimental import pallas as pl
from jax.experimental.pallas import tpu as pltpu
from jax.sharding import PartitionSpec as P

BLK = 128
PIECE = 256
HALF = PIECE // 2
HEAD = 16
LINK = jnp.int16
FINE = 64.0
TOP = 14.9
MESH = pl.DeviceIdType.MESH
NT = (((1,), (1,)), ((), ()))


def encode(value):
    most = jnp.maximum(jnp.max(jnp.abs(value), axis=0, keepdims=True), 1e-30)
    power = jnp.ceil(jnp.log2(most) * FINE)
    scaled = jnp.round(value * jnp.exp2(TOP - power / FINE))
    head = jnp.broadcast_to(power, (HEAD, value.shape[1]))
    return head.astype(jnp.int32).astype(LINK), scaled.astype(jnp.int32).astype(LINK)


def decode(head, scaled):
    power = head.astype(jnp.int32).astype(jnp.float32)[0:1, :]
    return scaled.astype(jnp.int32).astype(jnp.float32) * jnp.exp2(power / FINE - TOP)


def kernel(n, n_row, coupling, factor, mask, out, left, right, partial, held, sent,
           col_send, col_recv, row_send, row_recv, ring_send, ring_recv):
    groups, order, width = coupling.shape
    share = out.shape[0]
    pieces = width // PIECE
    scen, row, col = lax.axis_index("scen"), lax.axis_index("row"), lax.axis_index("col")

    half = n // 2
    side, depth = lax.rem(scen, 2), scen // 2
    place = jnp.where(side == 0, depth, n - 1 - depth)

    def at(position):
        position = lax.rem(position + 2 * n, n)
        return jnp.where(position < half, 2 * position, 2 * (n - 1 - position) + 1)

    around = (at(place + 1), at(place - 1))
    partners = [lax.rem(row + n_row - d, n_row) for d in range(1, n_row)]
    barrier = pltpu.get_barrier_semaphore()
    for target in around:
        pl.semaphore_signal(barrier, inc=1, device_id=(target, row, col), device_id_type=MESH)
    for target in partners:
        pl.semaphore_signal(barrier, inc=1, device_id=(scen, target, col), device_id_type=MESH)
    pl.semaphore_signal(barrier, inc=1, device_id=(scen, row, 1 - col), device_id_type=MESH)

    mine = pl.ds(pl.multiple_of(col * width, width), width)
    col_copies, row_copies = [], []
    for g in range(groups):
        rows = []
        for i in range(order // BLK):
            rows.append(jnp.concatenate([
                coupling[g, i * BLK:(i + 1) * BLK, j * BLK:(j + 1) * BLK]
                * mask[g, i, j].astype(jnp.float32).astype(jnp.bfloat16)
                for j in range(width // BLK)], axis=1))
        masked = jnp.concatenate(rows, axis=0)
        solved = jnp.dot(factor[g], masked, preferred_element_type=jnp.float32)
        left[g, mine, :] = solved.T.astype(jnp.bfloat16)
        if g == 0:
            pl.semaphore_wait(barrier, 2 + n_row)
        copy = pltpu.make_async_remote_copy(
            src_ref=left.at[g, mine], dst_ref=left.at[g, mine],
            send_sem=col_send.at[g], recv_sem=col_recv.at[g],
            device_id=(scen, row, 1 - col), device_id_type=MESH)
        copy.start()
        col_copies.append(copy)
    for k in range(pieces):
        for d in range(1, n_row):
            copy = pltpu.make_async_remote_copy(
                src_ref=left.at[:, pl.ds(pl.multiple_of(col * width + k * PIECE, PIECE), PIECE)],
                dst_ref=right.at[d - 1, :, pl.ds(k * PIECE, PIECE)],
                send_sem=row_send.at[d - 1, k], recv_sem=row_recv.at[d - 1, k],
                device_id=(scen, partners[d - 1], col), device_id_type=MESH)
            copy.start()
            row_copies.append(copy)

    ring_copies = {}

    def multiply(phase):
        d, k = phase // pieces, phase % pieces
        if d == 0:
            def block(g):
                return left[g, pl.ds(pl.multiple_of(col * width + k * PIECE, PIECE), PIECE), :]
        else:
            row_copies[k * (n_row - 1) + d - 1].wait_recv()

            def block(g):
                return right[d - 1, g, k * PIECE:(k + 1) * PIECE, :]

        @pl.loop(0, 2)
        def _(b):
            rows = pl.ds(pl.multiple_of(b * width, width), width)
            total = lax.dot_general(left[0, rows, :], block(0), NT, preferred_element_type=jnp.float32)
            for g in range(1, groups):
                total += lax.dot_general(left[g, rows, :], block(g), NT, preferred_element_type=jnp.float32)
            partial[phase, pl.ds(b * half, half)] = total.reshape(half, share, PIECE)

    def hop(phase, way, step):
        lanes = slice(way * HALF, (way + 1) * HALF)
        chunk = at(place - 1 - step) if way == 0 else at(place + 1 + step)
        value = partial[phase, chunk, :, lanes]
        if step:
            ring_copies[phase, way, step - 1].wait_recv()
            value += decode(held[phase, way, step - 1, 0:HEAD, :], held[phase, way, step - 1, HEAD:, :])
        if step == n - 1:
            d, k = phase // pieces, phase % pieces
            start = lax.rem(row + d, n_row) * width + k * PIECE + way * HALF
            out[:, pl.ds(pl.multiple_of(start, HALF), HALF)] = value
            return
        head, scaled = encode(value)
        sent[phase, way, step, 0:HEAD, :] = head
        sent[phase, way, step, HEAD:, :] = scaled
        copy = pltpu.make_async_remote_copy(
            src_ref=sent.at[phase, way, step], dst_ref=held.at[phase, way, step],
            send_sem=ring_send.at[phase, way, step], recv_sem=ring_recv.at[phase, way, step],
            device_id=(around[way], row, col), device_id_type=MESH)
        copy.start()
        ring_copies[phase, way, step] = copy

    for copy in col_copies:
        copy.wait_recv()
    starts = [0] * pieces + [n - 2 + 5 * (i // (n_row - 1)) for i in range(pieces * (n_row - 1))]
    order_of = list(range(pieces)) + [d * pieces + k for k in range(pieces) for d in range(1, n_row)]
    for tick in range(max(starts) + n):
        for phase, start in zip(order_of, starts):
            step = tick - start
            if step == 0:
                multiply(phase)
            if 0 <= step < n:
                hop(phase, 0, step)
                hop(phase, 1, step)
    for copy in col_copies + row_copies + list(ring_copies.values()):
        copy.wait_send()


def fused(n, n_row, coupling, factor_inv, block_mask):
    groups, order, width = coupling.shape
    rows = 2 * width
    share = rows // n
    phases = n_row * width // PIECE
    message = (phases, 2, n - 1, HEAD + share, HALF)
    vmem = pl.BlockSpec(memory_space=pltpu.VMEM)
    tile = pl.pallas_call(
        functools.partial(kernel, n, n_row),
        out_shape=jax.ShapeDtypeStruct((share, n_row * width), jnp.float32),
        in_specs=[vmem, vmem, pl.BlockSpec(memory_space=pltpu.SMEM)],
        out_specs=vmem,
        scratch_shapes=[
            pltpu.VMEM((groups, rows, order), jnp.bfloat16),
            pltpu.VMEM((n_row - 1, groups, width, order), jnp.bfloat16),
            pltpu.VMEM((phases, n, share, PIECE), jnp.float32),
            pltpu.VMEM(message, LINK),
            pltpu.VMEM(message, LINK),
            pltpu.SemaphoreType.DMA((groups,)),
            pltpu.SemaphoreType.DMA((groups,)),
            pltpu.SemaphoreType.DMA((n_row - 1, width // PIECE)),
            pltpu.SemaphoreType.DMA((n_row - 1, width // PIECE)),
            pltpu.SemaphoreType.DMA(message[:3]),
            pltpu.SemaphoreType.DMA(message[:3]),
        ],
        compiler_params=pltpu.CompilerParams(
            collective_id=0, has_side_effects=True, vmem_limit_bytes=60 * 1024 * 1024),
    )(coupling, factor_inv, block_mask)
    return tile.reshape(1, share, n_row, 1, width)


def plain(coupling, factor_inv, block_mask):
    groups, order, width = coupling.shape
    spread = jnp.broadcast_to(
        block_mask[:, :, None, :, None], (groups, order // BLK, BLK, width // BLK, BLK)
    )
    masked = coupling * spread.reshape(groups, order, width).astype(jnp.bfloat16)
    solved = jnp.einsum(
        "snk,skw->snw", factor_inv, masked, preferred_element_type=jnp.float32
    ).astype(jnp.bfloat16)
    left = lax.all_gather(solved, "col", axis=2, tiled=True)
    share = left.shape[2] // lax.axis_size("scen")
    tile = lax.dot_general(
        left,
        lax.all_gather(solved, "row", axis=2, tiled=True),
        (((0, 1), (0, 1)), ((), ())),
        preferred_element_type=jnp.float32,
    )
    summed = lax.psum_scatter(tile, "scen", scatter_dimension=0, tiled=True)
    return summed.reshape(1, share, summed.shape[1] // width, 1, width)


def solution(mesh):
    n, n_row = mesh.shape["scen"], mesh.shape["row"]

    def shards(coupling, factor_inv, block_mask):
        width = coupling.shape[2]
        share = 2 * width // n
        if share % 16 == 0 and width % PIECE == 0 and n % 2 == 0 and n > 2 and n_row > 1:
            return fused(n, n_row, coupling, factor_inv, block_mask)
        return plain(coupling, factor_inv, block_mask)

    in_specs = (
        P("scen", None, ("row", "col")),
        P("scen", None, None),
        P("scen", None, ("row", "col")),
    )
    out_specs = P("row", "scen", None, "col", None)
    return jax.shard_map(shards, mesh=mesh, in_specs=in_specs, out_specs=out_specs, check_vma=False)
```

```python
import functools

import jax
import jax.numpy as jnp
from jax import lax
from jax.experimental import pallas as pl
from jax.experimental.pallas import tpu as pltpu
from jax.sharding import PartitionSpec as P

BLK = 128
PIECE = 256
HALF = PIECE // 2
HEAD = 16
LINK = jnp.int16
FINE = 64.0
TOP = 14.9
STARTS = (4, 7, 9, 10)
MESH = pl.DeviceIdType.MESH
NT = (((1,), (1,)), ((), ()))


def encode(value):
    most = jnp.maximum(jnp.max(jnp.abs(value), axis=0, keepdims=True), 1e-30)
    power = jnp.ceil(jnp.log2(most) * FINE)
    scaled = jnp.round(value * jnp.exp2(TOP - power / FINE))
    head = jnp.broadcast_to(power, (HEAD, value.shape[1]))
    return head.astype(jnp.int32).astype(LINK), scaled.astype(jnp.int32).astype(LINK)


def decode(head, scaled):
    power = head.astype(jnp.int32).astype(jnp.float32)[0:1, :]
    return scaled.astype(jnp.int32).astype(jnp.float32) * jnp.exp2(power / FINE - TOP)


def kernel(n, n_row, coupling, factor, mask, out, left, right,
           col_send, col_recv, row_send, row_recv, ring_send, ring_recv, *buffers):
    groups, order, width = coupling.shape
    share = out.shape[0]
    phases = phases_of(n_row, width)
    partial, held, sent = [buffers[i * len(phases):(i + 1) * len(phases)] for i in range(3)]
    late = sorted({phase[1:3] for phase in phases if phase[0]})
    scen, row, col = lax.axis_index("scen"), lax.axis_index("row"), lax.axis_index("col")

    half = n // 2
    side, depth = lax.rem(scen, 2), scen // 2
    place = jnp.where(side == 0, depth, n - 1 - depth)

    def at(position):
        position = lax.rem(position + 2 * n, n)
        return jnp.where(position < half, 2 * position, 2 * (n - 1 - position) + 1)

    around = (at(place + 1), at(place - 1))
    partners = [lax.rem(row + n_row - d, n_row) for d in range(1, n_row)]
    barrier = pltpu.get_barrier_semaphore()
    for target in around:
        pl.semaphore_signal(barrier, inc=1, device_id=(target, row, col), device_id_type=MESH)
    for target in partners:
        pl.semaphore_signal(barrier, inc=1, device_id=(scen, target, col), device_id_type=MESH)
    pl.semaphore_signal(barrier, inc=1, device_id=(scen, row, 1 - col), device_id_type=MESH)

    mine = pl.ds(pl.multiple_of(col * width, width), width)
    col_copies, row_copies = [], {}

    def row_send_piece(g, k):
        base, count = late[k]
        for d in range(1, n_row):
            copy = pltpu.make_async_remote_copy(
                src_ref=left.at[g, pl.ds(pl.multiple_of(col * width + base, HALF), count)],
                dst_ref=right.at[d - 1, g, pl.ds(base, count)],
                send_sem=row_send.at[d - 1, k, g], recv_sem=row_recv.at[d - 1, k, g],
                device_id=(scen, partners[d - 1], col), device_id_type=MESH)
            copy.start()
            row_copies[d, base, g] = copy

    for g in range(groups):
        rows = []
        for i in range(order // BLK):
            rows.append(jnp.concatenate([
                coupling[g, i * BLK:(i + 1) * BLK, j * BLK:(j + 1) * BLK]
                * mask[g, i, j].astype(jnp.float32).astype(jnp.bfloat16)
                for j in range(width // BLK)], axis=1))
        masked = jnp.concatenate(rows, axis=0)
        solved = jnp.dot(factor[g], masked, preferred_element_type=jnp.float32)
        left[g, mine, :] = solved.T.astype(jnp.bfloat16)
        if g == 0:
            pl.semaphore_wait(barrier, 2 + n_row)
        copy = pltpu.make_async_remote_copy(
            src_ref=left.at[g, mine], dst_ref=left.at[g, mine],
            send_sem=col_send.at[g], recv_sem=col_recv.at[g],
            device_id=(scen, row, 1 - col), device_id_type=MESH)
        copy.start()
        col_copies.append(copy)
        row_send_piece(g, 0)
    for k in range(1, len(late)):
        for g in range(groups):
            row_send_piece(g, k)

    ring_copies = {}

    def multiply(phase, b):
        d, base, count, _ = phases[phase]

        def block(g):
            if d:
                return right[d - 1, g, base:base + count, :]
            return left[g, pl.ds(pl.multiple_of(col * width + base, HALF), count), :]

        rows = pl.ds(pl.multiple_of(b * width, width), width)
        total = lax.dot_general(left[0, rows, :], block(0), NT, preferred_element_type=jnp.float32)
        for g in range(1, groups):
            total += lax.dot_general(left[g, rows, :], block(g), NT, preferred_element_type=jnp.float32)
        partial[phase][pl.ds(b * half, half)] = total.reshape(half, share, count)

    def hop(phase, way, step):
        d, base, count, by_rows = phases[phase]
        if by_rows:
            rows, lanes = slice(way * share // 2, (way + 1) * share // 2), slice(0, count)
        else:
            rows, lanes = slice(0, share), slice(way * count // 2, (way + 1) * count // 2)
        chunk = at(place - 1 - step) if way == 0 else at(place + 1 + step)
        value = partial[phase][chunk, rows, lanes]
        if step:
            ring_copies[phase, way, step - 1].wait_recv()
            came = held[phase]
            value += decode(came[way, step - 1, 0:HEAD, :], came[way, step - 1, HEAD:, :])
        if step == n - 1:
            start = lax.rem(row + d, n_row) * width + base + lanes.start
            out[rows, pl.ds(pl.multiple_of(start, HALF), lanes.stop - lanes.start)] = value
            return
        head, scaled = encode(value)
        sent[phase][way, step, 0:HEAD, :] = head
        sent[phase][way, step, HEAD:, :] = scaled
        copy = pltpu.make_async_remote_copy(
            src_ref=sent[phase].at[way, step], dst_ref=held[phase].at[way, step],
            send_sem=ring_send.at[phase, way, step], recv_sem=ring_recv.at[phase, way, step],
            device_id=(around[way], row, col), device_id_type=MESH)
        copy.start()
        ring_copies[phase, way, step] = copy

    early = [phase for phase in range(len(phases)) if phases[phase][0] == 0]
    for phase in early:
        multiply(phase, col)
    for copy in col_copies:
        copy.wait_recv()
    starts = [0 if phase in early else STARTS[min(late.index(phases[phase][1:3]), len(STARTS) - 1)]
              for phase in range(len(phases))]
    for tick in range(max(starts) + n):
        for phase, start in enumerate(starts):
            step = tick - start
            if step == 0 and phase in early:
                multiply(phase, 1 - col)
            elif step == 0:
                d, base = phases[phase][:2]
                for g in range(groups):
                    row_copies[d, base, g].wait_recv()

                @pl.loop(0, 2)
                def _(b):
                    multiply(phase, b)
            if 0 <= step < n:
                hop(phase, 0, step)
                hop(phase, 1, step)
    for copy in col_copies + list(row_copies.values()) + list(ring_copies.values()):
        copy.wait_send()


def phases_of(n_row, width):
    early = [(0, base, PIECE, False) for base in range(0, width, PIECE)]
    late = [(base, PIECE, False) for base in range(0, width - PIECE, PIECE)]
    late += [(base, HALF, True) for base in (width - PIECE, width - HALF)]
    return early + [(d, *piece) for piece in late for d in range(1, n_row)]


def fused(n, n_row, coupling, factor_inv, block_mask):
    groups, order, width = coupling.shape
    rows = 2 * width
    share = rows // n
    phases = phases_of(n_row, width)
    late = len(phases) - width // PIECE
    shapes = [(2, n - 1, HEAD + (share // 2 if by_rows else share), HALF) for _, _, _, by_rows in phases]
    partials = [pltpu.VMEM((n, share, count), jnp.float32) for _, _, count, _ in phases]
    messages = [pltpu.VMEM(shape, LINK) for shape in shapes]
    vmem = pl.BlockSpec(memory_space=pltpu.VMEM)
    tile = pl.pallas_call(
        functools.partial(kernel, n, n_row),
        out_shape=jax.ShapeDtypeStruct((share, n_row * width), jnp.float32),
        in_specs=[vmem, vmem, pl.BlockSpec(memory_space=pltpu.SMEM)],
        out_specs=vmem,
        scratch_shapes=[
            pltpu.VMEM((groups, rows, order), jnp.bfloat16),
            pltpu.VMEM((n_row - 1, groups, width, order), jnp.bfloat16),
            pltpu.SemaphoreType.DMA((groups,)),
            pltpu.SemaphoreType.DMA((groups,)),
            pltpu.SemaphoreType.DMA((n_row - 1, late, groups)),
            pltpu.SemaphoreType.DMA((n_row - 1, late, groups)),
            pltpu.SemaphoreType.DMA((len(phases), 2, n - 1)),
            pltpu.SemaphoreType.DMA((len(phases), 2, n - 1)),
            *partials, *messages, *messages,
        ],
        compiler_params=pltpu.CompilerParams(
            collective_id=0, has_side_effects=True, vmem_limit_bytes=60 * 1024 * 1024),
    )(coupling, factor_inv, block_mask)
    return tile.reshape(1, share, n_row, 1, width)


def plain(coupling, factor_inv, block_mask):
    groups, order, width = coupling.shape
    spread = jnp.broadcast_to(
        block_mask[:, :, None, :, None], (groups, order // BLK, BLK, width // BLK, BLK)
    )
    masked = coupling * spread.reshape(groups, order, width).astype(jnp.bfloat16)
    solved = jnp.einsum(
        "snk,skw->snw", factor_inv, masked, preferred_element_type=jnp.float32
    ).astype(jnp.bfloat16)
    left = lax.all_gather(solved, "col", axis=2, tiled=True)
    share = left.shape[2] // lax.axis_size("scen")
    tile = lax.dot_general(
        left,
        lax.all_gather(solved, "row", axis=2, tiled=True),
        (((0, 1), (0, 1)), ((), ())),
        preferred_element_type=jnp.float32,
    )
    summed = lax.psum_scatter(tile, "scen", scatter_dimension=0, tiled=True)
    return summed.reshape(1, share, summed.shape[1] // width, 1, width)


def solution(mesh):
    n, n_row = mesh.shape["scen"], mesh.shape["row"]

    def shards(coupling, factor_inv, block_mask):
        width = coupling.shape[2]
        share = 2 * width // n
        if share % 32 == 0 and width % PIECE == 0 and n % 2 == 0 and n > 2 and n_row > 1:
            return fused(n, n_row, coupling, factor_inv, block_mask)
        return plain(coupling, factor_inv, block_mask)

    in_specs = (
        P("scen", None, ("row", "col")),
        P("scen", None, None),
        P("scen", None, ("row", "col")),
    )
    out_specs = P("row", "scen", None, "col", None)
    return jax.shard_map(shards, mesh=mesh, in_specs=in_specs, out_specs=out_specs, check_vma=False)
```
